32 devices in a mesh: grp: 2 (over y), vocab: 16 (over z, x, core).
Axes of the slice: x: 2, y: 2, z: 4, core: 2. Of those that a mesh axis runs over, the one named last changes fastest.
Arguments:
- doc_rows: bfloat16 [16384, 256], P(('grp', 'vocab')), may hold values from -6 to 6
- row_slot: int32 [16384], P(('grp', 'vocab')), may hold values from 0 to 1023, as said below
- word_table: bfloat16 [16, 2048, 256], P('vocab', 'grp'), may hold values from -0.75 to 0.75
- pos_tiles: int32 [2, 256], P(None, ('grp', 'vocab')), may hold values from 0 to 15, as said below
- pos_counts: int32 [256, 128, 128], P(('grp', 'vocab')), may hold values from 0 to 3
- neg_tiles: int32 [2, 3840], P(None, ('grp', 'vocab')), may hold values from 0 to 15, as said below
- live_tiles: int32 [2, 32], P(None, ('grp', 'vocab')), may hold values from 2 to 120, as said below
Outputs:
- doc_grad: float32 [16384, 256], P(('grp', 'vocab'))
- word_grad: float32 [16, 2048, 256], P('vocab', 'grp')
The draws below stay inside these ranges and needn't reach their ends.
Inputs may be any that keep to these rules, and one draw needn't show every extreme that they name: `row_slot`: A row's value is v * 64 + c for its vocabulary owner v and a slot c below 64; the values of one device's rows are distinct, so no owner gets more than 64 rows from one device, and in every device's rows some owner gets exactly 64. `pos_tiles`: row 0 is a document block below 8, row 1 a word block of the device's vocabulary slice below 16; only a device's first live tiles are used. `neg_tiles`: row 0 is a document block below 8, row 1 a word block of the device's vocabulary slice below 16; only a device's first live tiles are used. `live_tiles`: row 0 counts a device's live positive tiles, at most 8 and exactly 8 on some device; row 1 its live negative tiles, at most 120 and exactly 120 on some device.
All inputs are finite; a program needn't handle non-finite values.
Results may differ from the reference program's by a relative error of at most 0.0055.
Values may be sent and summed in bfloat16 or wider, within the bound.
A program may use at most 64 MiB of HBM per device.

```python
import jax
import jax.numpy as jnp
from jax import lax

E = 256
TILE = 128
DOC_DEV = 512
WORDS_DEV = 1024
POS_CAP = 8
NEG_CAP = 120
SLICE_WORDS = 2048
WBLOCKS = 16
DOCS = 16384
N_GRP = 2
N_VOCAB = 16


def tile_list(key, count):
    first, second, third = jax.random.split(key, 3)
    blocks = jax.random.randint(first, (count,), 0, 2 * DOC_DEV // TILE)
    raw = jax.random.randint(second, (count,), 0, WBLOCKS)
    order = jax.random.permutation(third, WBLOCKS)
    words = order[raw * raw // WBLOCKS]
    return jnp.stack([blocks, words]).astype(jnp.int32)


def draw_row_slot(key, part):
    cap = 2 * DOC_DEV // N_VOCAB

    def one_device(inner):
        first, second, third = jax.random.split(inner, 3)
        full = jax.random.randint(first, (), 0, N_VOCAB)
        others = jax.random.permutation(second, (N_VOCAB - 1) * cap)[:DOC_DEV - cap]
        owner = others // cap
        owner = owner + (owner >= full).astype(jnp.int32)
        values = jnp.concatenate([full * cap + jnp.arange(cap, dtype=jnp.int32), owner * cap + others % cap])
        return jax.random.permutation(third, values)
    keys = jax.random.split(jax.random.fold_in(key, 11), N_GRP * N_VOCAB)
    return jax.vmap(one_device)(keys).reshape(-1).astype(jnp.int32)


def draw_pos_tiles(key, part):
    return tile_list(jax.random.fold_in(key, 23), POS_CAP * N_GRP * N_VOCAB)


def draw_neg_tiles(key, part):
    return tile_list(jax.random.fold_in(key, 37), NEG_CAP * N_GRP * N_VOCAB)


def draw_live_tiles(key, part):
    first, second, third, fourth = jax.random.split(jax.random.fold_in(key, 53), 4)
    count = N_GRP * N_VOCAB
    positive = jax.random.randint(first, (count,), POS_CAP // 4, POS_CAP + 1)
    negative = jax.random.randint(second, (count,), NEG_CAP // 8, NEG_CAP // 3 + 1)
    positive = positive.at[jax.random.randint(third, (), 0, count)].set(POS_CAP)
    negative = negative.at[jax.random.randint(fourth, (), 0, count)].set(NEG_CAP)
    return jnp.stack([positive, negative]).astype(jnp.int32)


def plant(entries, stream_key, smallest, top_value):
    place = [jax.random.randint(jax.random.fold_in(stream_key, axis), (), 0, length) for axis, length in enumerate(entries.shape)]
    widest = entries.shape.index(max(entries.shape))
    neighbour = place[:widest] + [(place[widest] + 1) % entries.shape[widest]] + place[widest + 1:]
    return entries.at[tuple(place)].set(smallest).at[tuple(neighbour)].set(top_value)


def level_of(key, extent, pieces, smallest, high):
    def one(position, parts):
        steps = jax.random.uniform(jax.random.fold_in(jax.random.fold_in(key, 6), position), (parts,), jnp.float32, smallest / len(pieces), high / len(pieces))
        return jnp.repeat(jnp.exp(steps), extent[position] // parts).reshape((-1,) + (1,) * (len(extent) - position - 1))

    gain = one(*pieces[0])
    for cut in pieces[1:]:
        gain = gain * one(*cut)
    return gain


def centred(rng, shape, deviation, reach, cuts=(), kind=jnp.bfloat16):
    entries = jax.random.normal(rng, shape, jnp.float32) * deviation
    if len(cuts) > 0:
        entries = level_of(rng, shape, cuts, -0.22, 0.18) * entries
    return jnp.clip(entries, min=-reach, max=reach).astype(kind)


def setup_inputs(seed: int = 0) -> dict:
    arg_keys = jax.random.split(jax.random.key(seed), 8)
    doc_rows = centred(arg_keys[0], (DOCS, E), 1.0, 6.0, ((0, 32),))
    row_slot = draw_row_slot(jax.random.fold_in(arg_keys[7], 71), 0)
    word_table = centred(arg_keys[2], (N_VOCAB, SLICE_WORDS, E), 0.125, 0.75, ((0, 16), (1, 2)))
    pos_tiles = draw_pos_tiles(jax.random.fold_in(arg_keys[7], 71), 0)
    pos_counts = plant(jax.random.randint(arg_keys[4], (POS_CAP * N_GRP * N_VOCAB, TILE, TILE), 0, 4), jax.random.fold_in(arg_keys[4], 1), 0, 3).astype(jnp.int32)
    neg_tiles = draw_neg_tiles(jax.random.fold_in(arg_keys[7], 71), 0)
    live_tiles = draw_live_tiles(jax.random.fold_in(arg_keys[7], 71), 0)
    return {"doc_rows": doc_rows, "row_slot": row_slot, "word_table": word_table, "pos_tiles": pos_tiles, "pos_counts": pos_counts, "neg_tiles": neg_tiles, "live_tiles": live_tiles}


def tile_update(accs, docs, words, doc_row, word_row, weigh):
    doc_acc, word_acc = accs
    block_docs = lax.dynamic_slice_in_dim(docs, doc_row, TILE, 0)
    block_words = lax.dynamic_slice_in_dim(words, word_row, TILE, 0)
    scores = jnp.dot(block_docs, block_words.T, preferred_element_type=jnp.float32)
    grads = weigh(scores).astype(jnp.bfloat16)
    doc_part = lax.dynamic_slice_in_dim(doc_acc, doc_row, TILE, 0) + jnp.dot(grads, block_words, preferred_element_type=jnp.float32)
    word_part = lax.dynamic_slice_in_dim(word_acc, word_row, TILE, 0) + jnp.dot(grads.T, block_docs, preferred_element_type=jnp.float32)
    doc_acc = lax.dynamic_update_slice_in_dim(doc_acc, doc_part, doc_row, 0)
    word_acc = lax.dynamic_update_slice_in_dim(word_acc, word_part, word_row, 0)
    return (doc_acc, word_acc)


def device_step(own, words, pos_list, pos_cnt, neg_list, pos_live, neg_live):
    weight = TILE ** -0.5
    doc_zero = jnp.zeros(own.shape, jnp.float32)
    word_zero = jnp.zeros(words.shape, jnp.float32)

    def pos_step(i, accs):
        counts = pos_cnt[i].astype(jnp.float32)
        return tile_update(accs, own, words, pos_list[0, i] * TILE, pos_list[1, i] * TILE,
                           lambda s: counts * (jax.nn.sigmoid(s) - 1.0) * weight)

    def neg_step(i, accs):
        return tile_update(accs, own, words, neg_list[0, i] * TILE, neg_list[1, i] * TILE,
                           lambda s: jax.nn.sigmoid(s) * weight)

    accs = lax.fori_loop(0, pos_live, pos_step, (doc_zero, word_zero))
    return lax.fori_loop(0, neg_live, neg_step, accs)


def reference(doc_rows, row_slot, word_table, pos_tiles, pos_counts, neg_tiles, live_tiles):
    own_rows = 2 * DOC_DEV
    cap = own_rows // N_VOCAB
    slice_rows = WORDS_DEV * N_GRP
    devices = N_GRP * N_VOCAB
    docs = doc_rows.reshape(devices, DOC_DEV, E)
    slots = row_slot.reshape(devices, DOC_DEV).astype(jnp.int32)
    placed = jax.vmap(lambda d, s: jnp.zeros((own_rows, E), doc_rows.dtype).at[s].set(d))(docs, slots)
    placed = placed.reshape(N_GRP, N_VOCAB, N_VOCAB, cap, E).transpose(2, 0, 1, 3, 4).reshape(N_VOCAB, N_GRP, own_rows, E)
    pos_list = pos_tiles.reshape(2, N_GRP, N_VOCAB, POS_CAP).transpose(2, 1, 0, 3)
    pos_cnt = pos_counts.reshape(N_GRP, N_VOCAB, POS_CAP, TILE, TILE).transpose(1, 0, 2, 3, 4)
    neg_list = neg_tiles.reshape(2, N_GRP, N_VOCAB, NEG_CAP).transpose(2, 1, 0, 3)
    live = live_tiles.reshape(2, N_GRP, N_VOCAB).transpose(2, 1, 0)

    def one_slice(inputs):
        own_v, words_v, plist_v, pcnt_v, nlist_v, live_v = inputs

        def one_group(total, item):
            own_g, plist_g, pcnt_g, nlist_g, live_g = item
            doc_part, word_part = device_step(own_g, words_v, plist_g, pcnt_g, nlist_g, live_g[0], live_g[1])
            rounded = lax.optimization_barrier(word_part.astype(jnp.bfloat16)).astype(jnp.float32)
            return total + rounded, doc_part

        total, doc_parts = lax.scan(one_group, jnp.zeros((slice_rows, E), jnp.float32),
                                    (own_v, plist_v, pcnt_v, nlist_v, live_v))
        return total, doc_parts

    word_grad, doc_parts = lax.map(one_slice, (placed, word_table, pos_list, pos_cnt, neg_list, live))
    back = doc_parts.reshape(N_VOCAB, N_GRP, N_VOCAB, cap, E).transpose(1, 2, 0, 3, 4).reshape(devices, own_rows, E)
    doc_grad = jnp.take_along_axis(back, slots[:, :, None], axis=1).reshape(devices * DOC_DEV, E)
    return (doc_grad, word_grad)
```

```python
import functools

import jax
import jax.numpy as jnp
from jax import lax
from jax.experimental import pallas as pl
from jax.experimental.pallas import tpu as pltpu
from jax.sharding import PartitionSpec as P

TILE = 128
SPLIT = 4
BF = jnp.bfloat16
F32 = jnp.float32
I32 = jnp.int32
MESH = pl.DeviceIdType.MESH


def nt(a, b):
    return lax.dot_general(a, b, (((1,), (1,)), ((), ())), preferred_element_type=F32)


def nn(a, b):
    return jnp.dot(a, b, preferred_element_type=F32)


def iota(shape, dim):
    return lax.broadcasted_iota(I32, shape, dim)


def step_kernel(
    n_grp,
    n_vocab,
    pos_hbm,
    live_hbm,
    slot_hbm,
    rows_hbm,
    table_hbm,
    neg_hbm,
    cnt_hbm,
    doc_out,
    word_out,
    pos_ref,
    live_ref,
    slot_ref,
    rows_ref,
    neg_ref,
    cnt_ref,
    outgoing,
    owned,
    words,
    hot_ref,
    n_ref,
    g_ref,
    dacc,
    dpart,
    back,
    wpart,
    wrecv,
    l_sem,
    d_send,
    d_recv,
    b_send,
    b_recv,
    w_send,
    w_recv,
    p_send,
    p_recv,
):
    g, v = lax.axis_index("grp"), lax.axis_index("vocab")
    own_rows, emb = owned.shape
    cols = words.shape[0]
    half = table_hbm.shape[0]
    cap = own_rows // n_vocab
    blocks, wblocks = own_rows // TILE, cols // TILE
    slots = neg_ref.shape[1]
    rows = rows_ref.shape[0]
    sub = half // SPLIT
    wide = 2 * TILE
    per = wide // cap
    z = v // per

    def peer_v(j):
        return lax.rem(v + j, n_vocab)

    def peer_g(j):
        return lax.rem(g + j, n_grp)

    def chunk(u):
        return pl.ds(pl.multiple_of(u * cap, cap), cap)

    def piece(u, q, n=1):
        return pl.ds(pl.multiple_of(u * half + q * sub, sub), n * sub)

    def doc_copy(u, src):
        return pltpu.make_async_remote_copy(
            outgoing.at[chunk(u)], owned.at[chunk(src)], d_send.at[u], d_recv.at[src], (g, u), MESH
        )

    def back_copy(u, src):
        return pltpu.make_async_remote_copy(
            dpart.at[chunk(u)], back.at[chunk(src)], b_send.at[u], b_recv.at[src], (g, u), MESH
        )

    def word_copy(u, src, q):
        return pltpu.make_async_remote_copy(
            table_hbm.at[pl.ds(q * sub, sub)],
            words.at[piece(src, q)],
            w_send.at[u, q],
            w_recv.at[src, q],
            (u, v),
            MESH,
        )

    def part_copy(u, src, q):
        r = pl.ds(q * sub, sub)
        return pltpu.make_async_remote_copy(
            wpart.at[u, r], wrecv.at[src, r], p_send.at[u, q], p_recv.at[src, q], (u, v), MESH
        )

    def each(n, body):
        if n == 2:
            body(1)
        else:
            lax.fori_loop(1, n, lambda j, c: (body(j), c)[1], 0)

    def loop(n, body):
        lax.fori_loop(0, n, lambda j, c: (body(j), c)[1], 0)

    def wide_block(k):
        b = lax.rem(z // 2 + k // 2, 2) * 2 + lax.rem(z + k, 2)
        return b, pl.ds(pl.multiple_of(b * wide, wide), wide)

    def pair_block(k):
        b = lax.rem(z // 2 + k, 2)
        return b, pl.ds(pl.multiple_of(b * 2 * wide, 2 * wide), 2 * wide)

    def others(k, body):
        b, _ = wide_block(k)

        def one(i):
            u = b * per + i
            if k == 0:
                pl.when(u != v)(lambda: body(u))
            else:
                body(u)

        loop(per, one)

    barrier = pltpu.get_barrier_semaphore()
    each(n_vocab, lambda j: pl.semaphore_signal(barrier, 1, device_id=(g, peer_v(j)), device_id_type=MESH))
    each(n_grp, lambda j: pl.semaphore_signal(barrier, 1, device_id=(peer_g(j), v), device_id_type=MESH))

    own_words = words.at[pl.ds(pl.multiple_of(g * half, half), half)]
    pairs_in = [
        (slot_hbm, slot_ref),
        (rows_hbm, rows_ref),
        (pos_hbm, pos_ref),
        (live_hbm, live_ref),
        (neg_hbm, neg_ref),
        (cnt_hbm, cnt_ref),
        (table_hbm, own_words),
    ]
    loads = [pltpu.make_async_copy(a, b, l_sem.at[i]) for i, (a, b) in enumerate(pairs_in)]
    for load in loads:
        load.start()

    pl.semaphore_wait(barrier, n_vocab + n_grp - 2)
    for q in range(SPLIT):
        each(n_grp, lambda j: word_copy(peer_g(j), g, q).start())

    loads[0].wait()
    loads[1].wait()

    for h in range(2):
        b, r = pair_block(h)
        put = iota((2 * wide, rows), 0) + b * 2 * wide == slot_ref[...]
        outgoing[r, :] = nn(jnp.where(put, 0.5, 0.0).astype(BF), rows_ref[...]).astype(BF)
        for k in (2 * h, 2 * h + 1):
            others(k, lambda u: doc_copy(u, v).start())
    owned[chunk(v), :] = outgoing[chunk(v), :]

    for load in loads[2:]:
        load.wait()
    alive = iota((blocks, slots), 1) < live_ref[0, 1]
    b_hot = (iota((blocks, slots), 0) == neg_ref[0:1, :]) & alive
    w_hot = iota((wblocks, slots), 0) == neg_ref[1:2, :]
    pairs = nt(b_hot.astype(F32).astype(BF), w_hot.astype(F32).astype(BF))
    spread = iota((wblocks, cols), 1) // TILE == iota((wblocks, cols), 0)
    n_ref[...] = nn(pairs.astype(BF), spread.astype(F32).astype(BF))

    n_pos = cnt_ref.shape[0]

    def counts(b, carry):
        flags = [
            jnp.where((pos_ref[0, i] == b) & (i < live_ref[0, 0]), pos_ref[1, i], wblocks) for i in range(n_pos)
        ]
        r = pl.ds(pl.multiple_of(b * TILE, TILE), TILE)

        def column(w, inner):
            total = jnp.zeros((TILE, TILE), F32)
            for i in range(n_pos):
                hit = jnp.where(flags[i] == w, 1.0, 0.0).astype(F32)
                total = total + cnt_ref[i].astype(F32) * jnp.full((TILE, TILE), hit, F32)
            g_ref[r, pl.ds(pl.multiple_of(w * TILE, TILE), TILE)] = total.astype(BF)
            return inner

        return lax.fori_loop(0, wblocks, column, carry)

    lax.fori_loop(0, blocks, counts, 0)

    slot_col = jnp.broadcast_to(slot_ref[...], (TILE, rows)).T
    for k in range(0, own_rows, TILE):
        hit = slot_col == iota(slot_col.shape, 1) + k
        hot_ref[:, k : k + TILE] = hit.astype(F32).astype(BF)

    scale = 0.5 * TILE ** (-0.5)
    last = SPLIT - 1

    def weigh(block, c):
        b, r = block
        tiles = r.size // TILE
        t = jnp.tanh(nt(owned[r, :], words[c, :]))
        n = jnp.concatenate(
            [jnp.broadcast_to(n_ref[pl.ds(tiles * b + k, 1), c], (TILE, c.size)) for k in range(tiles)], axis=0
        )
        cnt = g_ref[r, c].astype(F32)
        g_ref[r, c] = (t * (n + cnt) + (n - cnt)).astype(BF)

    def landed(k):
        others(k, lambda u: doc_copy(u, u).wait_recv())

    def arrived(q):
        each(n_grp, lambda j: word_copy(peer_g(j), peer_g(j), q).wait_recv())

    def far(block, q, n=1):
        each(n_grp, lambda j: weigh(block, piece(peer_g(j), q, n)))

    def begin(block):
        r = block[1]
        dacc[r, :] = nn(g_ref[r, near], words[near, :])

        def more(j):
            c = piece(peer_g(j), 0, last)
            dacc[r, :] += nn(g_ref[r, c], words[c, :])

        each(n_grp, more)

    def finish(block):
        far(block, last)
        r = block[1]

        def more(j):
            c = piece(peer_g(j), last)
            dacc[r, :] += nn(g_ref[r, c], words[c, :])

        each(n_grp, more)
        dpart[r, :] = (dacc[r, :] * scale).astype(BF)

    def word_part(u, q, n=1):
        lhs = g_ref[:, piece(u, q, n)]
        grad = lax.dot_general(lhs, owned[...], (((0,), (0,)), ((), ())), preferred_element_type=F32)
        return (grad * (2 * scale)).astype(BF)

    def send_parts(q, n):
        def one(j):
            u = peer_g(j)
            wpart[u, q * sub : (q + n) * sub, :] = word_part(u, q, n)
            for i in range(q, q + n):
                part_copy(u, g, i).start()

        each(n_grp, one)

    near = pl.ds(pl.multiple_of(g * half, half), half)
    first, second = pair_block(0), pair_block(1)
    third, fourth = wide_block(2), wide_block(3)

    landed(0)
    landed(1)
    weigh(first, near)
    arrived(0)
    arrived(1)
    far(first, 0, 2)
    landed(2)
    weigh(third, near)
    far(third, 0, 2)
    arrived(2)
    far(first, 2)
    far(third, 2)
    begin(first)
    begin(third)
    landed(3)
    weigh(fourth, near)
    far(fourth, 0, last)
    begin(fourth)
    for q in range(SPLIT):
        each(n_grp, lambda j: word_copy(peer_g(j), g, q).wait_send())
    send_parts(0, 1)
    arrived(last)
    finish(first)
    for k in (0, 1):
        others(k, lambda u: back_copy(u, v).start())
    finish(second)
    for k in (2, 3):
        others(k, lambda u: back_copy(u, v).start())
    send_parts(1, last)
    word_out[...] = word_part(g, 0, SPLIT).astype(F32)
    back[chunk(v), :] = dpart[chunk(v), :]

    for k in range(4):
        others(k, lambda u: back_copy(u, u).wait_recv())
        if k == 1:
            r = first[1]
            doc_out[...] = nn(hot_ref[:, r], back[r, :])
        if k > 1:
            r = wide_block(k)[1]
            doc_out[...] += nn(hot_ref[:, r], back[r, :])

    for q in range(SPLIT):
        r = pl.ds(q * sub, sub)

        def add(j):
            u = peer_g(j)
            part_copy(u, u, q).wait_recv()
            word_out[r, :] += wrecv[u, r, :].astype(F32)

        each(n_grp, add)

    each(n_vocab, lambda j: doc_copy(peer_v(j), v).wait_send())
    each(n_vocab, lambda j: back_copy(peer_v(j), v).wait_send())
    for q in range(SPLIT):
        each(n_grp, lambda j: part_copy(peer_g(j), g, q).wait_send())


def store_kernel(doc_ref, word_ref, doc_out, word_out, sem):
    a = pltpu.make_async_copy(doc_ref, doc_out, sem.at[0])
    b = pltpu.make_async_copy(word_ref, word_out.at[0], sem.at[1])
    b.start()
    a.start()
    a.wait()
    b.wait()


def local(doc_rows, row_slot, word_table, pos_tiles, pos_counts, neg_tiles, live_tiles):
    n_grp, n_vocab = lax.axis_size("grp"), lax.axis_size("vocab")
    rows, emb = doc_rows.shape
    own_rows = 2 * rows
    half = word_table.shape[1]
    cols = half * n_grp
    hbm = pl.BlockSpec(memory_space=pltpu.HBM)
    vmem = pl.BlockSpec(memory_space=pltpu.VMEM)
    dma = pltpu.SemaphoreType.DMA
    slots = row_slot.reshape(1, rows)
    live = live_tiles.T
    args = (pos_tiles, live, slots, doc_rows, word_table[0], neg_tiles, pos_counts)
    doc, word = pl.pallas_call(
        functools.partial(step_kernel, n_grp, n_vocab),
        out_shape=(jax.ShapeDtypeStruct((rows, emb), F32), jax.ShapeDtypeStruct((half, emb), F32)),
        in_specs=[hbm] * 7,
        out_specs=(vmem, vmem),
        scratch_shapes=[
            pltpu.SMEM(pos_tiles.shape, I32),
            pltpu.SMEM(live.shape, I32),
            pltpu.VMEM((1, rows), I32),
            pltpu.VMEM((rows, emb), BF),
            pltpu.VMEM(neg_tiles.shape, I32),
            pltpu.VMEM(pos_counts.shape, I32),
            pltpu.VMEM((own_rows, emb), BF),
            pltpu.VMEM((own_rows, emb), BF),
            pltpu.VMEM((cols, emb), BF),
            pltpu.VMEM((rows, own_rows), BF),
            pltpu.VMEM((own_rows // TILE, cols), F32),
            pltpu.VMEM((own_rows, cols), BF),
            pltpu.VMEM((own_rows, emb), F32),
            pltpu.VMEM((own_rows, emb), BF),
            pltpu.VMEM((own_rows, emb), BF),
            pltpu.VMEM((n_grp, half, emb), BF),
            pltpu.VMEM((n_grp, half, emb), BF),
            dma((7,)),
            dma((n_vocab,)),
            dma((n_vocab,)),
            dma((n_vocab,)),
            dma((n_vocab,)),
            dma((n_grp, SPLIT)),
            dma((n_grp, SPLIT)),
            dma((n_grp, SPLIT)),
            dma((n_grp, SPLIT)),
        ],
        compiler_params=pltpu.CompilerParams(collective_id=0, has_side_effects=True, vmem_limit_bytes=44 << 20),
    )(*[pltpu.with_memory_space_constraint(x, pltpu.HBM) for x in args])
    return pl.pallas_call(
        store_kernel,
        out_shape=(jax.ShapeDtypeStruct((rows, emb), F32), jax.ShapeDtypeStruct((1, half, emb), F32)),
        in_specs=[vmem, vmem],
        out_specs=(hbm, hbm),
        scratch_shapes=[dma((2,))],
        compiler_params=pltpu.CompilerParams(vmem_limit_bytes=8 << 20),
    )(doc, word)


def solution(mesh):
    placed = (
        P(("grp", "vocab"), None),
        P(("grp", "vocab")),
        P("vocab", "grp", None),
        P(None, ("grp", "vocab")),
        P(("grp", "vocab"), None, None),
        P(None, ("grp", "vocab")),
        P(None, ("grp", "vocab")),
    )
    return jax.shard_map(
        local,
        mesh=mesh,
        in_specs=placed,
        out_specs=(P(("grp", "vocab"), None), P("vocab", "grp", None)),
        check_vma=False,
    )
```

```python
import functools

import jax
import jax.numpy as jnp
from jax import lax
from jax.experimental import pallas as pl
from jax.experimental.pallas import tpu as pltpu
from jax.sharding import PartitionSpec as P

TILE = 128
SPLIT = 4
BF = jnp.bfloat16
F32 = jnp.float32
I32 = jnp.int32
MESH = pl.DeviceIdType.MESH


def nt(a, b):
    return lax.dot_general(a, b, (((1,), (1,)), ((), ())), preferred_element_type=F32)


def nn(a, b):
    return jnp.dot(a, b, preferred_element_type=F32)


def iota(shape, dim):
    return lax.broadcasted_iota(I32, shape, dim)


def step_kernel(
    n_grp,
    n_vocab,
    pos_hbm,
    live_hbm,
    slot_hbm,
    rows_hbm,
    table_hbm,
    neg_hbm,
    cnt_hbm,
    doc_out,
    word_out,
    pos_ref,
    live_ref,
    slot_ref,
    rows_ref,
    neg_ref,
    cnt_ref,
    outgoing,
    owned,
    words,
    hot_ref,
    counts,
    which_vec,
    which_ref,
    neg_vec,
    n_ref,
    g_ref,
    dacc,
    dpart,
    back,
    wpart,
    wrecv,
    l_sem,
    t_sem,
    d_send,
    d_recv,
    b_send,
    b_recv,
    w_send,
    w_recv,
    p_send,
    p_recv,
):
    g, v = lax.axis_index("grp"), lax.axis_index("vocab")
    own_rows, emb = owned.shape
    cols = words.shape[0]
    half = table_hbm.shape[0]
    cap = own_rows // n_vocab
    blocks, wblocks = own_rows // TILE, cols // TILE
    slots = neg_ref.shape[1]
    lanes = which_vec.shape[1]
    rows = rows_ref.shape[0]
    sub = half // SPLIT
    wide = 2 * TILE
    per = wide // cap
    z = v // per

    def peer_v(j):
        return lax.rem(v + j, n_vocab)

    def peer_g(j):
        return lax.rem(g + j, n_grp)

    def chunk(u):
        return pl.ds(pl.multiple_of(u * cap, cap), cap)

    def piece(u, q, n=1):
        return pl.ds(pl.multiple_of(u * half + q * sub, sub), n * sub)

    def doc_copy(u, src):
        return pltpu.make_async_remote_copy(
            outgoing.at[chunk(u)], owned.at[chunk(src)], d_send.at[u], d_recv.at[src], (g, u), MESH
        )

    def back_copy(u, src):
        return pltpu.make_async_remote_copy(
            dpart.at[chunk(u)], back.at[chunk(src)], b_send.at[u], b_recv.at[src], (g, u), MESH
        )

    def word_copy(u, src, q):
        return pltpu.make_async_remote_copy(
            table_hbm.at[pl.ds(q * sub, sub)],
            words.at[piece(src, q)],
            w_send.at[u, q],
            w_recv.at[src, q],
            (u, v),
            MESH,
        )

    def part_copy(u, src, q):
        r = pl.ds(q * sub, sub)
        return pltpu.make_async_remote_copy(
            wpart.at[u, r], wrecv.at[src, r], p_send.at[u, q], p_recv.at[src, q], (u, v), MESH
        )

    def each(n, body):
        if n == 2:
            body(1)
        else:
            lax.fori_loop(1, n, lambda j, c: (body(j), c)[1], 0)

    def loop(n, body):
        lax.fori_loop(0, n, lambda j, c: (body(j), c)[1], 0)

    def wide_block(k):
        b = lax.rem(z // 2 + k // 2, 2) * 2 + lax.rem(z + k, 2)
        return b, pl.ds(pl.multiple_of(b * wide, wide), wide)

    def pair_block(k):
        b = lax.rem(z // 2 + k, 2)
        return b, pl.ds(pl.multiple_of(b * 2 * wide, 2 * wide), 2 * wide)

    def others(k, body):
        b, _ = wide_block(k)

        def one(i):
            u = b * per + i
            if k == 0:
                pl.when(u != v)(lambda: body(u))
            else:
                body(u)

        loop(per, one)

    barrier = pltpu.get_barrier_semaphore()
    each(n_vocab, lambda j: pl.semaphore_signal(barrier, 1, device_id=(g, peer_v(j)), device_id_type=MESH))
    each(n_grp, lambda j: pl.semaphore_signal(barrier, 1, device_id=(peer_g(j), v), device_id_type=MESH))

    own_words = words.at[pl.ds(pl.multiple_of(g * half, half), half)]
    pairs_in = [
        (slot_hbm, slot_ref),
        (rows_hbm, rows_ref),
        (pos_hbm, pos_ref),
        (live_hbm, live_ref),
        (neg_hbm, neg_ref),
        (cnt_hbm, cnt_ref),
        (table_hbm, own_words),
    ]
    loads = [pltpu.make_async_copy(a, b, l_sem.at[i]) for i, (a, b) in enumerate(pairs_in)]
    for load in loads:
        load.start()

    pl.semaphore_wait(barrier, n_vocab + n_grp - 2)
    for q in range(SPLIT):
        each(n_grp, lambda j: word_copy(peer_g(j), g, q).start())

    loads[0].wait()
    loads[1].wait()

    for h in range(2):
        b, r = pair_block(h)
        put = iota((2 * wide, rows), 0) + b * 2 * wide == slot_ref[...]
        outgoing[r, :] = nn(jnp.where(put, 0.5, 0.0).astype(BF), rows_ref[...]).astype(BF)
        for k in (2 * h, 2 * h + 1):
            others(k, lambda u: doc_copy(u, v).start())
    owned[chunk(v), :] = outgoing[chunk(v), :]

    for load in loads[2:]:
        load.wait()
    alive = iota((blocks, slots), 1) < live_ref[0, 1]
    b_hot = (iota((blocks, slots), 0) == neg_ref[0:1, :]) & alive
    w_hot = iota((lanes, slots), 0) == neg_ref[1:2, :]
    neg_vec[...] = nt(b_hot.astype(F32).astype(BF), w_hot.astype(F32).astype(BF))
    n_pos = cnt_ref.shape[0]
    keys = [jnp.where(i < live_ref[0, 0], pos_ref[0, i] * wblocks + pos_ref[1, i], -1) for i in range(n_pos)]
    place = iota((blocks, lanes), 0) * wblocks + iota((blocks, lanes), 1)
    which = jnp.full((blocks, lanes), n_pos, I32)
    for i in range(n_pos):
        which = jnp.where(place == keys[i], i, which)
    which_vec[...] = which
    tables = [
        pltpu.make_async_copy(which_vec, which_ref, t_sem.at[0]),
        pltpu.make_async_copy(neg_vec, n_ref, t_sem.at[1]),
    ]
    for table in tables:
        table.start()
    tile_cnt = [cnt_ref[i].astype(F32) for i in range(n_pos)]
    for i in range(n_pos):
        total = tile_cnt[i]
        for k in range(n_pos):
            if k != i:
                same = jnp.where(keys[k] == keys[i], 1.0, 0.0).astype(F32)
                total = total + tile_cnt[k] * same
        counts[i] = total
    counts[n_pos] = jnp.zeros((TILE, TILE), F32)
    for table in tables:
        table.wait()

    slot_col = jnp.broadcast_to(slot_ref[...], (TILE, rows)).T
    for k in range(0, own_rows, TILE):
        hit = slot_col == iota(slot_col.shape, 1) + k
        hot_ref[:, k : k + TILE] = hit.astype(F32).astype(BF)

    scale = 0.5 * TILE ** (-0.5)
    last, early = SPLIT - 1, SPLIT // 2

    def weigh(block, c):
        b, r = block
        tiles = r.size // TILE
        t = jnp.tanh(nt(owned[r, :], words[c, :]))
        for k in range(tiles):
            for w in range(c.size // TILE):
                sel = pl.ds(pl.multiple_of(c.start + w * TILE, TILE), TILE)
                at = (tiles * b + k, c.start // TILE + w)
                n, cnt = n_ref[at], counts[which_ref[at]]
                s = t[k * TILE : (k + 1) * TILE, w * TILE : (w + 1) * TILE]
                out = pl.ds(pl.multiple_of(r.start + k * TILE, TILE), TILE)
                g_ref[out, sel] = (s * (n + cnt) + (n - cnt)).astype(BF)

    def landed(k):
        others(k, lambda u: doc_copy(u, u).wait_recv())

    def arrived(q):
        each(n_grp, lambda j: word_copy(peer_g(j), peer_g(j), q).wait_recv())

    def far(block, q, n=1):
        each(n_grp, lambda j: weigh(block, piece(peer_g(j), q, n)))

    def begin(block):
        r = block[1]
        dacc[r, :] = nn(g_ref[r, near], words[near, :])

        def more(j):
            c = piece(peer_g(j), 0, early)
            dacc[r, :] += nn(g_ref[r, c], words[c, :])

        each(n_grp, more)

    def finish(block):
        far(block, last)
        r = block[1]

        def more(j):
            c = piece(peer_g(j), early, SPLIT - early)
            dacc[r, :] += nn(g_ref[r, c], words[c, :])

        each(n_grp, more)
        dpart[r, :] = (dacc[r, :] * scale).astype(BF)

    def word_part(u, q, n=1):
        lhs = g_ref[:, piece(u, q, n)]
        grad = lax.dot_general(lhs, owned[...], (((0,), (0,)), ((), ())), preferred_element_type=F32)
        return (grad * (2 * scale)).astype(BF)

    def send_parts(q, n):
        def one(j):
            u = peer_g(j)
            wpart[u, q * sub : (q + n) * sub, :] = word_part(u, q, n)
            for i in range(q, q + n):
                part_copy(u, g, i).start()

        each(n_grp, one)

    near = pl.ds(pl.multiple_of(g * half, half), half)
    first, second = pair_block(0), pair_block(1)
    third, fourth = wide_block(2), wide_block(3)
    whole = (0, pl.ds(0, own_rows))

    def gather(k):
        others(k, lambda u: back_copy(u, u).wait_recv())
        r = wide_block(k)[1]
        doc_out[...] += nn(hot_ref[:, r], back[r, :])

    def add_parts(q):
        r = pl.ds(q * sub, sub)

        def one(j):
            u = peer_g(j)
            part_copy(u, u, q).wait_recv()
            word_out[r, :] += wrecv[u, r, :].astype(F32)

        each(n_grp, one)

    landed(0)
    landed(1)
    weigh(first, near)
    arrived(0)
    arrived(1)
    far(first, 0, early)
    begin(first)
    landed(2)
    weigh(third, near)
    far(third, 0, early)
    landed(3)
    far(fourth, 0)
    send_parts(0, 1)
    weigh(fourth, near)
    far(fourth, 1, early - 1)
    begin(second)
    for q in range(early, last):
        arrived(q)
        far(whole, q)
    arrived(last)
    finish(second)
    for k in (2, 3):
        others(k, lambda u: back_copy(u, v).start())
    finish(first)
    for k in (0, 1):
        others(k, lambda u: back_copy(u, v).start())
    send_parts(1, last)
    word_out[...] = word_part(g, 0, SPLIT).astype(F32)
    back[chunk(v), :] = dpart[chunk(v), :]

    for k in (0, 1):
        others(k, lambda u: back_copy(u, u).wait_recv())
    r = first[1]
    doc_out[...] = nn(hot_ref[:, r], back[r, :])
    for q in range(last):
        add_parts(q)
    gather(2)
    gather(3)
    add_parts(last)

    each(n_vocab, lambda j: doc_copy(peer_v(j), v).wait_send())
    each(n_vocab, lambda j: back_copy(peer_v(j), v).wait_send())
    for q in range(SPLIT):
        each(n_grp, lambda j: word_copy(peer_g(j), g, q).wait_send())
        each(n_grp, lambda j: part_copy(peer_g(j), g, q).wait_send())


def store_kernel(doc_ref, word_ref, doc_out, word_out, sem):
    a = pltpu.make_async_copy(doc_ref, doc_out, sem.at[0])
    b = pltpu.make_async_copy(word_ref, word_out.at[0], sem.at[1])
    b.start()
    a.start()
    a.wait()
    b.wait()


def local(doc_rows, row_slot, word_table, pos_tiles, pos_counts, neg_tiles, live_tiles):
    n_grp, n_vocab = lax.axis_size("grp"), lax.axis_size("vocab")
    rows, emb = doc_rows.shape
    own_rows = 2 * rows
    half = word_table.shape[1]
    cols = half * n_grp
    lanes = pl.cdiv(cols // TILE, TILE) * TILE
    hbm = pl.BlockSpec(memory_space=pltpu.HBM)
    vmem = pl.BlockSpec(memory_space=pltpu.VMEM)
    dma = pltpu.SemaphoreType.DMA
    slots = row_slot.reshape(1, rows)
    live = live_tiles.T
    args = (pos_tiles, live, slots, doc_rows, word_table[0], neg_tiles, pos_counts)
    doc, word = pl.pallas_call(
        functools.partial(step_kernel, n_grp, n_vocab),
        out_shape=(jax.ShapeDtypeStruct((rows, emb), F32), jax.ShapeDtypeStruct((half, emb), F32)),
        in_specs=[hbm] * 7,
        out_specs=(vmem, vmem),
        scratch_shapes=[
            pltpu.SMEM(pos_tiles.shape, I32),
            pltpu.SMEM(live.shape, I32),
            pltpu.VMEM((1, rows), I32),
            pltpu.VMEM((rows, emb), BF),
            pltpu.VMEM(neg_tiles.shape, I32),
            pltpu.VMEM(pos_counts.shape, I32),
            pltpu.VMEM((own_rows, emb), BF),
            pltpu.VMEM((own_rows, emb), BF),
            pltpu.VMEM((cols, emb), BF),
            pltpu.VMEM((rows, own_rows), BF),
            pltpu.VMEM((pos_counts.shape[0] + 1, TILE, TILE), F32),
            pltpu.VMEM((own_rows // TILE, lanes), I32),
            pltpu.SMEM((own_rows // TILE, lanes), I32),
            pltpu.VMEM((own_rows // TILE, lanes), F32),
            pltpu.SMEM((own_rows // TILE, lanes), F32),
            pltpu.VMEM((own_rows, cols), BF),
            pltpu.VMEM((own_rows, emb), F32),
            pltpu.VMEM((own_rows, emb), BF),
            pltpu.VMEM((own_rows, emb), BF),
            pltpu.VMEM((n_grp, half, emb), BF),
            pltpu.VMEM((n_grp, half, emb), BF),
            dma((7,)),
            dma((2,)),
            dma((n_vocab,)),
            dma((n_vocab,)),
            dma((n_vocab,)),
            dma((n_vocab,)),
            dma((n_grp, SPLIT)),
            dma((n_grp, SPLIT)),
            dma((n_grp, SPLIT)),
            dma((n_grp, SPLIT)),
        ],
        compiler_params=pltpu.CompilerParams(collective_id=0, has_side_effects=True, vmem_limit_bytes=44 << 20),
    )(*[pltpu.with_memory_space_constraint(x, pltpu.HBM) for x in args])
    return pl.pallas_call(
        store_kernel,
        out_shape=(jax.ShapeDtypeStruct((rows, emb), F32), jax.ShapeDtypeStruct((1, half, emb), F32)),
        in_specs=[vmem, vmem],
        out_specs=(hbm, hbm),
        scratch_shapes=[dma((2,))],
        compiler_params=pltpu.CompilerParams(vmem_limit_bytes=8 << 20),
    )(doc, word)


def solution(mesh):
    placed = (
        P(("grp", "vocab"), None),
        P(("grp", "vocab")),
        P("vocab", "grp", None),
        P(None, ("grp", "vocab")),
        P(("grp", "vocab"), None, None),
        P(None, ("grp", "vocab")),
        P(None, ("grp", "vocab")),
    )
    return jax.shard_map(
        local,
        mesh=mesh,
        in_specs=placed,
        out_specs=(P(("grp", "vocab"), None), P("vocab", "grp", None)),
        check_vma=False,
    )
```

```python
import functools

import jax
import jax.numpy as jnp
from jax import lax
from jax.experimental import pallas as pl
from jax.experimental.pallas import tpu as pltpu
from jax.sharding import PartitionSpec as P

TILE = 128
SPLIT = 4
BF = jnp.bfloat16
F32 = jnp.float32
I32 = jnp.int32
MESH = pl.DeviceIdType.MESH


def nt(a, b):
    return lax.dot_general(a, b, (((1,), (1,)), ((), ())), preferred_element_type=F32)


def nn(a, b):
    return jnp.dot(a, b, preferred_element_type=F32)


def iota(shape, dim):
    return lax.broadcasted_iota(I32, shape, dim)


def step_kernel(
    n_grp,
    n_vocab,
    pos_hbm,
    live_hbm,
    slot_hbm,
    rows_hbm,
    table_hbm,
    neg_hbm,
    cnt_hbm,
    doc_out,
    word_out,
    pos_ref,
    live_ref,
    slot_ref,
    rows_ref,
    neg_ref,
    cnt_ref,
    outgoing,
    owned,
    words,
    hot_ref,
    counts,
    which_vec,
    which_ref,
    neg_vec,
    n_ref,
    g_ref,
    dacc,
    dpart,
    back,
    wpart,
    wrecv,
    l_sem,
    t_sem,
    d_send,
    d_recv,
    b_send,
    b_recv,
    w_send,
    w_recv,
    p_send,
    p_recv,
):
    g, v = lax.axis_index("grp"), lax.axis_index("vocab")
    own_rows, emb = owned.shape
    cols = words.shape[0]
    half = table_hbm.shape[0]
    cap = own_rows // n_vocab
    blocks, wblocks = own_rows // TILE, cols // TILE
    slots = neg_ref.shape[1]
    lanes = which_vec.shape[1]
    rows = rows_ref.shape[0]
    sub = half // SPLIT
    wide = 2 * TILE
    per = wide // cap
    z = v // per

    def peer_v(j):
        return lax.rem(v + j, n_vocab)

    def peer_g(j):
        return lax.rem(g + j, n_grp)

    def chunk(u):
        return pl.ds(pl.multiple_of(u * cap, cap), cap)

    def piece(u, q, n=1):
        return pl.ds(pl.multiple_of(u * half + q * sub, sub), n * sub)

    def doc_copy(u, src):
        return pltpu.make_async_remote_copy(
            outgoing.at[chunk(u)], owned.at[chunk(src)], d_send.at[u], d_recv.at[src], (g, u), MESH
        )

    def back_copy(u, src):
        return pltpu.make_async_remote_copy(
            dpart.at[chunk(u)], back.at[chunk(src)], b_send.at[u], b_recv.at[src], (g, u), MESH
        )

    def word_copy(u, src, q):
        return pltpu.make_async_remote_copy(
            table_hbm.at[pl.ds(q * sub, sub)],
            words.at[piece(src, q)],
            w_send.at[u, q],
            w_recv.at[src, q],
            (u, v),
            MESH,
        )

    def part_copy(u, src, q):
        r = pl.ds(q * sub, sub)
        return pltpu.make_async_remote_copy(
            wpart.at[u, r], wrecv.at[src, r], p_send.at[u, q], p_recv.at[src, q], (u, v), MESH
        )

    def each(n, body):
        if n == 2:
            body(1)
        else:
            lax.fori_loop(1, n, lambda j, c: (body(j), c)[1], 0)

    def loop(n, body):
        lax.fori_loop(0, n, lambda j, c: (body(j), c)[1], 0)

    def wide_block(k):
        b = lax.rem(z // 2 + k // 2, 2) * 2 + lax.rem(z + k, 2)
        return b, pl.ds(pl.multiple_of(b * wide, wide), wide)

    def pair_block(k):
        b = lax.rem(z // 2 + k, 2)
        return b, pl.ds(pl.multiple_of(b * 2 * wide, 2 * wide), 2 * wide)

    def others(k, body):
        b, _ = wide_block(k)

        def one(i):
            u = b * per + i
            if k == 0:
                pl.when(u != v)(lambda: body(u))
            else:
                body(u)

        loop(per, one)

    barrier = pltpu.get_barrier_semaphore()
    each(n_vocab, lambda j: pl.semaphore_signal(barrier, 1, device_id=(g, peer_v(j)), device_id_type=MESH))
    each(n_grp, lambda j: pl.semaphore_signal(barrier, 1, device_id=(peer_g(j), v), device_id_type=MESH))

    own_words = words.at[pl.ds(pl.multiple_of(g * half, half), half)]
    pairs_in = [
        (slot_hbm, slot_ref),
        (rows_hbm, rows_ref),
        (pos_hbm, pos_ref),
        (live_hbm, live_ref),
        (neg_hbm, neg_ref),
        (cnt_hbm, cnt_ref),
        (table_hbm, own_words),
    ]
    loads = [pltpu.make_async_copy(a, b, l_sem.at[i]) for i, (a, b) in enumerate(pairs_in)]
    for load in loads:
        load.start()

    pl.semaphore_wait(barrier, n_vocab + n_grp - 2)
    for q in range(SPLIT):
        each(n_grp, lambda j: word_copy(peer_g(j), g, q).start())

    loads[0].wait()
    loads[1].wait()

    for h in range(2):
        b, r = pair_block(h)
        put = iota((2 * wide, rows), 0) + b * 2 * wide == slot_ref[...]
        outgoing[r, :] = nn(jnp.where(put, 0.5, 0.0).astype(BF), rows_ref[...]).astype(BF)
        for k in (2 * h, 2 * h + 1):
            others(k, lambda u: doc_copy(u, v).start())
    owned[chunk(v), :] = outgoing[chunk(v), :]

    for load in loads[2:]:
        load.wait()
    alive = iota((blocks, slots), 1) < live_ref[0, 1]
    b_hot = (iota((blocks, slots), 0) == neg_ref[0:1, :]) & alive
    w_hot = iota((lanes, slots), 0) == neg_ref[1:2, :]
    neg_vec[...] = nt(b_hot.astype(F32).astype(BF), w_hot.astype(F32).astype(BF))
    n_pos = cnt_ref.shape[0]
    keys = [jnp.where(i < live_ref[0, 0], pos_ref[0, i] * wblocks + pos_ref[1, i], -1) for i in range(n_pos)]
    place = iota((blocks, lanes), 0) * wblocks + iota((blocks, lanes), 1)
    which = jnp.full((blocks, lanes), n_pos, I32)
    for i in range(n_pos):
        which = jnp.where(place == keys[i], i, which)
    which_vec[...] = which
    tables = [
        pltpu.make_async_copy(which_vec, which_ref, t_sem.at[0]),
        pltpu.make_async_copy(neg_vec, n_ref, t_sem.at[1]),
    ]
    for table in tables:
        table.start()
    tile_cnt = [cnt_ref[i].astype(F32) for i in range(n_pos)]
    for i in range(n_pos):
        total = tile_cnt[i]
        for k in range(n_pos):
            if k != i:
                same = jnp.where(keys[k] == keys[i], 1.0, 0.0).astype(F32)
                total = total + tile_cnt[k] * same
        counts[i] = total
    counts[n_pos] = jnp.zeros((TILE, TILE), F32)
    for table in tables:
        table.wait()

    slot_col = jnp.broadcast_to(slot_ref[...], (TILE, rows)).T
    for k in range(0, own_rows, TILE):
        hit = slot_col == iota(slot_col.shape, 1) + k
        hot_ref[:, k : k + TILE] = hit.astype(F32).astype(BF)

    scale = 0.5 * TILE ** (-0.5)
    last, early = SPLIT - 1, SPLIT // 2

    def weigh(block, c):
        b, r = block
        tiles = r.size // TILE
        t = jnp.tanh(nt(owned[r, :], words[c, :]))
        for k in range(tiles):
            for w in range(c.size // TILE):
                sel = pl.ds(pl.multiple_of(c.start + w * TILE, TILE), TILE)
                at = (tiles * b + k, c.start // TILE + w)
                n, cnt = n_ref[at], counts[which_ref[at]]
                s = t[k * TILE : (k + 1) * TILE, w * TILE : (w + 1) * TILE]
                out = pl.ds(pl.multiple_of(r.start + k * TILE, TILE), TILE)
                g_ref[out, sel] = (s * (n + cnt) + (n - cnt)).astype(BF)

    def landed(k):
        others(k, lambda u: doc_copy(u, u).wait_recv())

    def arrived(q):
        each(n_grp, lambda j: word_copy(peer_g(j), peer_g(j), q).wait_recv())

    def far(block, q, n=1):
        each(n_grp, lambda j: weigh(block, piece(peer_g(j), q, n)))

    def begin(block):
        r = block[1]
        dacc[r, :] = nn(g_ref[r, near], words[near, :])

        def more(j):
            c = piece(peer_g(j), 0, early)
            dacc[r, :] += nn(g_ref[r, c], words[c, :])

        each(n_grp, more)

    def finish(block):
        far(block, last)
        r = block[1]

        def more(j):
            c = piece(peer_g(j), early, SPLIT - early)
            dacc[r, :] += nn(g_ref[r, c], words[c, :])

        each(n_grp, more)
        dpart[r, :] = (dacc[r, :] * scale).astype(BF)

    def word_part(u, q, n=1):
        lhs = g_ref[:, piece(u, q, n)]
        grad = lax.dot_general(lhs, owned[...], (((0,), (0,)), ((), ())), preferred_element_type=F32)
        return (grad * (2 * scale)).astype(BF)

    def send_parts(q, n):
        def one(j):
            u = peer_g(j)
            wpart[u, q * sub : (q + n) * sub, :] = word_part(u, q, n)
            for i in range(q, q + n):
                part_copy(u, g, i).start()

        each(n_grp, one)

    near = pl.ds(pl.multiple_of(g * half, half), half)
    first, second = pair_block(0), pair_block(1)
    third, fourth = wide_block(2), wide_block(3)
    whole = (0, pl.ds(0, own_rows))

    def add_parts(q):
        r = pl.ds(q * sub, sub)

        def one(j):
            u = peer_g(j)
            part_copy(u, u, q).wait_recv()
            word_out[r, :] += wrecv[u, r, :].astype(F32)

        each(n_grp, one)

    landed(0)
    landed(1)
    weigh(first, near)
    arrived(0)
    arrived(1)
    far(first, 0, early)
    begin(first)
    landed(2)
    weigh(third, near)
    far(third, 0, early)
    landed(3)
    far(fourth, 0)
    weigh(fourth, near)
    far(fourth, 1, early - 1)
    begin(second)
    for q in range(early, last):
        arrived(q)
        far(whole, q)
    send_parts(0, 1)
    arrived(last)
    finish(second)
    for k in (2, 3):
        others(k, lambda u: back_copy(u, v).start())
    finish(first)
    for k in (0, 1):
        others(k, lambda u: back_copy(u, v).start())
    send_parts(1, last)
    word_out[...] = word_part(g, 0, SPLIT).astype(F32)
    back[chunk(v), :] = dpart[chunk(v), :]

    for k in (0, 1):
        others(k, lambda u: back_copy(u, u).wait_recv())
    r = first[1]
    doc_out[...] = nn(hot_ref[:, r], back[r, :])
    for q in range(last):
        add_parts(q)
    for k in (2, 3):
        others(k, lambda u: back_copy(u, u).wait_recv())
    r = second[1]
    doc_out[...] += nn(hot_ref[:, r], back[r, :])
    add_parts(last)

    each(n_vocab, lambda j: doc_copy(peer_v(j), v).wait_send())
    each(n_vocab, lambda j: back_copy(peer_v(j), v).wait_send())
    for q in range(SPLIT):
        each(n_grp, lambda j: word_copy(peer_g(j), g, q).wait_send())
        each(n_grp, lambda j: part_copy(peer_g(j), g, q).wait_send())


def store_kernel(doc_ref, word_ref, doc_out, word_out, sem):
    a = pltpu.make_async_copy(doc_ref, doc_out, sem.at[0])
    b = pltpu.make_async_copy(word_ref, word_out.at[0], sem.at[1])
    b.start()
    a.start()
    a.wait()
    b.wait()


def local(doc_rows, row_slot, word_table, pos_tiles, pos_counts, neg_tiles, live_tiles):
    n_grp, n_vocab = lax.axis_size("grp"), lax.axis_size("vocab")
    rows, emb = doc_rows.shape
    own_rows = 2 * rows
    half = word_table.shape[1]
    cols = half * n_grp
    lanes = pl.cdiv(cols // TILE, TILE) * TILE
    hbm = pl.BlockSpec(memory_space=pltpu.HBM)
    vmem = pl.BlockSpec(memory_space=pltpu.VMEM)
    dma = pltpu.SemaphoreType.DMA
    slots = row_slot.reshape(1, rows)
    live = live_tiles.T
    args = (pos_tiles, live, slots, doc_rows, word_table[0], neg_tiles, pos_counts)
    doc, word = pl.pallas_call(
        functools.partial(step_kernel, n_grp, n_vocab),
        out_shape=(jax.ShapeDtypeStruct((rows, emb), F32), jax.ShapeDtypeStruct((half, emb), F32)),
        in_specs=[hbm] * 7,
        out_specs=(vmem, vmem),
        scratch_shapes=[
            pltpu.SMEM(pos_tiles.shape, I32),
            pltpu.SMEM(live.shape, I32),
            pltpu.VMEM((1, rows), I32),
            pltpu.VMEM((rows, emb), BF),
            pltpu.VMEM(neg_tiles.shape, I32),
            pltpu.VMEM(pos_counts.shape, I32),
            pltpu.VMEM((own_rows, emb), BF),
            pltpu.VMEM((own_rows, emb), BF),
            pltpu.VMEM((cols, emb), BF),
            pltpu.VMEM((rows, own_rows), BF),
            pltpu.VMEM((pos_counts.shape[0] + 1, TILE, TILE), F32),
            pltpu.VMEM((own_rows // TILE, lanes), I32),
            pltpu.SMEM((own_rows // TILE, lanes), I32),
            pltpu.VMEM((own_rows // TILE, lanes), F32),
            pltpu.SMEM((own_rows // TILE, lanes), F32),
            pltpu.VMEM((own_rows, cols), BF),
            pltpu.VMEM((own_rows, emb), F32),
            pltpu.VMEM((own_rows, emb), BF),
            pltpu.VMEM((own_rows, emb), BF),
            pltpu.VMEM((n_grp, half, emb), BF),
            pltpu.VMEM((n_grp, half, emb), BF),
            dma((7,)),
            dma((2,)),
            dma((n_vocab,)),
            dma((n_vocab,)),
            dma((n_vocab,)),
            dma((n_vocab,)),
            dma((n_grp, SPLIT)),
            dma((n_grp, SPLIT)),
            dma((n_grp, SPLIT)),
            dma((n_grp, SPLIT)),
        ],
        compiler_params=pltpu.CompilerParams(collective_id=0, has_side_effects=True, vmem_limit_bytes=44 << 20),
    )(*[pltpu.with_memory_space_constraint(x, pltpu.HBM) for x in args])
    return pl.pallas_call(
        store_kernel,
        out_shape=(jax.ShapeDtypeStruct((rows, emb), F32), jax.ShapeDtypeStruct((1, half, emb), F32)),
        in_specs=[vmem, vmem],
        out_specs=(hbm, hbm),
        scratch_shapes=[dma((2,))],
        compiler_params=pltpu.CompilerParams(vmem_limit_bytes=8 << 20),
    )(doc, word)


def solution(mesh):
    placed = (
        P(("grp", "vocab"), None),
        P(("grp", "vocab")),
        P("vocab", "grp", None),
        P(None, ("grp", "vocab")),
        P(("grp", "vocab"), None, None),
        P(None, ("grp", "vocab")),
        P(None, ("grp", "vocab")),
    )
    return jax.shard_map(
        local,
        mesh=mesh,
        in_specs=placed,
        out_specs=(P(("grp", "vocab"), None), P("vocab", "grp", None)),
        check_vma=False,
    )
```
